32 devices in a mesh: cells: 8 (over z, x), vel: 4 (over y, core).
Axes of the slice: x: 2, y: 2, z: 4, core: 2. Of those that a mesh axis runs over, the one named last changes fastest.
Arguments:
- dist: float32 [32768, 32, 128], P('vel', 'cells'), may hold values from 0.05 to 2
- basis: float32 [512, 32768], P(None, 'vel'), may hold values from -0.03125 to 0.03125
- left_factor: float32 [2048, 512], P('vel'), may hold values from -0.25 to 0.25
- right_factor: float32 [2048, 512], P('vel'), may hold values from -0.25 to 0.25
- mixing: float32 [512, 2048], P(None, 'vel'), may hold values from -0.125 to 0.125
- next_cell: int32 [32, 128], P('cells'), may hold values from 0 to 127, as said below
- prev_cell: int32 [32, 128], P('cells'), may hold values from 0 to 127, as said below
- cell_kind: int32 [32, 128], P('cells'), may hold values 0 or 1
Outputs:
- relaxed: float32 [32768, 32, 128], P('vel', 'cells')
The draws below stay inside these ranges and needn't reach their ends.
Inputs may be any that keep to these rules, and one draw needn't show every extreme that they name: In each column x, following next_cell[x, y] from any row visits all 128 rows once before returning. prev_cell[x, next_cell[x, y]] = y for every cell.
All inputs are finite; a program needn't handle non-finite values. No bound on the sum of `cell_kind` on one device may be relied on, other than what follows from the above.
Results may differ from the reference program's by a relative error of at most 0.0003.
Values sent between devices are 32-bit elements; how exact they have to be, the bound alone decides.
A program may use at most 192 MiB of HBM per device.

```python
import math
import jax
import jax.numpy as jnp
from jax import lax

NV1 = 32
K = 512
R = 2048
TY = 128
V = 32768
NX = 32
N_VEL = 4


def cycle_tables(key):
    base = jax.random.fold_in(key, 11)
    keys = jax.random.split(base, NX)
    orders = jax.vmap(lambda single: jax.random.permutation(single, TY))(keys).astype(jnp.int32)
    columns = jnp.broadcast_to(jnp.arange(NX, dtype=jnp.int32)[:, None], (NX, TY))
    following = jnp.roll(orders, -1, axis=1)
    preceding = jnp.roll(orders, 1, axis=1)
    forward = jnp.zeros((NX, TY), jnp.int32).at[columns, orders].set(following)
    backward = jnp.zeros((NX, TY), jnp.int32).at[columns, orders].set(preceding)
    return (forward, backward)


def draw_next_cell(key, part):
    return cycle_tables(key)[0]


def draw_prev_cell(key, part):
    return cycle_tables(key)[1]


def touch_ends(entries, rng, smallest, top_value):
    index_at = [jax.random.randint(jax.random.fold_in(rng, axis), (), 0, length) for axis, length in enumerate(entries.shape)]
    widest = entries.shape.index(max(entries.shape))
    next_to = index_at[:widest] + [(index_at[widest] + 1) % entries.shape[widest]] + index_at[widest + 1:]
    return entries.at[tuple(index_at)].set(smallest).at[tuple(next_to)].set(top_value)


def levels(rng, dims, pieces, low, largest):
    level = 1.0
    for axis_at, shards_of in pieces:
        steps = jax.random.uniform(jax.random.fold_in(jax.random.fold_in(rng, 6), axis_at), (shards_of,), jnp.float32, low / len(pieces), largest / len(pieces))
        level = level * jnp.repeat(jnp.exp(steps), dims[axis_at] // shards_of).reshape((-1,) + (1,) * (len(dims) - 1 - axis_at))
    return level


def bell_draw(own_key, shape, deviation, most, pieces=(), held_as=jnp.bfloat16):
    level = levels(own_key, shape, pieces, -0.22, 0.18) if pieces else 1.0
    values = jax.random.normal(own_key, shape, jnp.float32) * deviation * level
    return jnp.minimum(jnp.maximum(values, -most), most).astype(held_as)


def setup_inputs(seed: int = 0) -> dict:
    splits = jax.random.split(jax.random.key(seed), 9)
    return {
        "dist": jnp.clip(jnp.exp(math.log(2.0) - 3.6888794 * jax.random.uniform(splits[0], (V, NX, TY), jnp.float32) ** levels(splits[0], (V, NX, TY), ((0, 4), (1, 8)), -0.2, 0.2)), 0.05, 2.0),
        "basis": bell_draw(splits[1], (K, V), V ** -0.5, 0.03125, ((1, 4),), jnp.float32),
        "left_factor": bell_draw(splits[2], (R, K), K ** -0.5, 0.25, ((0, 4),), jnp.float32),
        "right_factor": bell_draw(splits[3], (R, K), K ** -0.5, 0.25, ((0, 4),), jnp.float32),
        "mixing": bell_draw(splits[4], (K, R), R ** -0.5, 0.125, ((1, 4),), jnp.float32),
        "next_cell": draw_next_cell(jax.random.fold_in(splits[8], 71), 0),
        "prev_cell": draw_prev_cell(jax.random.fold_in(splits[8], 71), 0),
        "cell_kind": touch_ends((jax.random.randint(splits[7], (NX, TY), 0, 6) < 1).astype(jnp.int32), jax.random.fold_in(splits[7], 1), 0, 1),
    }


SPEED_RANGE = 6.4
RATIO_X = 0.2
RATIO_Y = 0.12
HALF_STEP = 0.5


def minmod(first, second):
    return 0.5 * (jnp.sign(first) + jnp.sign(second)) * jnp.minimum(jnp.abs(first), jnp.abs(second))


def face_flux(upwind, behind, ahead, courant):
    return courant * (upwind + 0.5 * (1.0 - jnp.abs(courant)) * minmod(upwind - behind, ahead - upwind))


def components(grid_index, points):
    plane = points * points
    index_x = grid_index // plane
    index_y = (grid_index // points) % points
    step = SPEED_RANGE / points
    middle = (points - 1) * 0.5
    return (index_x.astype(jnp.float32) - middle) * step, (index_y.astype(jnp.float32) - middle) * step


def x_divergence(padded, courant):
    width = padded.shape[1] - 4
    speed = courant[:, None, None]
    forward = face_flux(padded[:, 1:width + 2], padded[:, 0:width + 1], padded[:, 2:width + 3], speed)
    backward = face_flux(padded[:, 2:width + 3], padded[:, 3:width + 4], padded[:, 1:width + 2], speed)
    flux = jnp.where(speed > 0, forward, backward)
    return flux[:, 1:] - flux[:, :-1]


def pick_rows(values, index):
    return jnp.take_along_axis(values, jnp.broadcast_to(index[None], values.shape), axis=2)


def y_divergence(field, courant, following, preceding):
    speed = courant[:, None, None]
    above = pick_rows(field, following)
    below = pick_rows(field, preceding)
    above_two = pick_rows(above, following)
    forward = face_flux(field, below, above, speed)
    backward = face_flux(above, above_two, field, speed)
    flux = jnp.where(speed > 0, forward, backward)
    return flux - pick_rows(flux, preceding)


def reference(dist, basis, left_factor, right_factor, mixing, next_cell, prev_cell, cell_kind):
    total, extent_x, extent_y = dist.shape
    per_device = total // N_VEL
    half = per_device // 2
    glob = jnp.arange(total, dtype=jnp.int32)
    owner = glob // per_device
    local = glob % per_device
    grid_index = jnp.where(local < half, owner * half + local, total - 1 - (owner * half + local - half))
    speed_x, speed_y = components(grid_index, NV1)
    courant_x = (speed_x * RATIO_X).reshape(N_VEL, per_device)
    courant_y = (speed_y * RATIO_Y).reshape(N_VEL, per_device)
    fluid = (1 - cell_kind).astype(jnp.float32)
    blocks = dist.reshape(N_VEL, per_device, extent_x, extent_y)
    basis_blocks = basis.reshape(basis.shape[0], N_VEL, per_device).transpose(1, 0, 2)

    def transported(block, cxb, cyb):
        padded = jnp.concatenate([block[:, -2:], block, block[:, :2]], axis=1)
        return block - fluid * (x_divergence(padded, cxb) + y_divergence(block, cyb, next_cell, prev_cell))

    def accumulate(carry, items):
        block, cxb, cyb, piece = items
        moved = transported(block, cxb, cyb).reshape(per_device, extent_x * extent_y)
        return carry + jnp.dot(piece, moved, precision=lax.Precision.HIGHEST, preferred_element_type=jnp.float32), None

    start = jnp.zeros((basis.shape[0], extent_x * extent_y), jnp.float32)
    moments, _ = lax.scan(accumulate, start, (blocks, courant_x, courant_y, basis_blocks))
    first = jnp.dot(left_factor, moments, precision=lax.Precision.HIGHEST, preferred_element_type=jnp.float32)
    second = jnp.dot(right_factor, moments, precision=lax.Precision.HIGHEST, preferred_element_type=jnp.float32)
    collision = jnp.dot(mixing, first * second, precision=lax.Precision.HIGHEST, preferred_element_type=jnp.float32)

    def rebuild(items):
        block, cxb, cyb, piece = items
        moved = transported(block, cxb, cyb)
        gain = jnp.dot(piece.T, collision, precision=lax.Precision.HIGHEST, preferred_element_type=jnp.float32)
        return moved + HALF_STEP * fluid * gain.reshape(moved.shape)

    relaxed = lax.map(rebuild, (blocks, courant_x, courant_y, basis_blocks))
    return relaxed.reshape(dist.shape)
```

```python
import functools

import jax
import jax.numpy as jnp
from jax import lax
from jax.experimental import pallas as pl
from jax.experimental.pallas import tpu as pltpu
from jax.sharding import PartitionSpec as P

NV1 = 32
SPEED_RANGE = 6.4
RATIO_X = 0.2
RATIO_Y = 0.12
HALF_STEP = 0.5
IN_FLIGHT = 3
BLOCK = NV1 * NV1 // 2


def shifted(x, by):
    size = lax.axis_size("cells")
    return lax.ppermute(x, "cells", [(i, (i + by) % size) for i in range(size)])


def minmod(a, b):
    return jnp.maximum(jnp.minimum(a, b), 0.0) + jnp.minimum(jnp.maximum(a, b), 0.0)


def split(x):
    high = x.astype(jnp.bfloat16)
    low = (x - high.astype(jnp.float32)).astype(jnp.bfloat16)
    return high, low


def dot(a, b):
    return jnp.dot(a, b, preferred_element_type=jnp.float32)


def difference(far, near, here, ahead, factor):
    step = here - near
    return (here + factor * minmod(step, ahead - here)) - (
        near + factor * minmod(near - far, step)
    )


def transport_kernel(upper, half, total, owner_ref, far, near, here, ahead, basis, table, fluid, moved_ref, mom_ref):
    i = pl.program_id(0)
    start = owner_ref[0] * half + i * BLOCK
    points = NV1
    middle = (points - 1) * 0.5
    step = SPEED_RANGE / points
    rows = lax.broadcasted_iota(jnp.int32, here.shape, 0) // points
    if upper:
        first = total - 1 - start
        index_y = (first // points) % points - rows
    else:
        first = start
        index_y = (first // points) % points + rows
    index_x = first // (points * points)
    cx = jnp.abs((index_x.astype(jnp.float32) - middle) * step * RATIO_X)
    cy = jnp.abs((index_y.astype(jnp.float32) - middle) * (step * RATIO_Y))
    u = here[...]
    high, low = split(u)
    picked = dot(jnp.concatenate([high, low], axis=1), table[0])
    cells = u.shape[1]
    near_y = picked[:, :cells]
    far_y = picked[:, cells : 2 * cells]
    ahead_y = picked[:, 2 * cells :]
    div_x = cx * difference(far[...], near[...], u, ahead[...], 0.5 * (1.0 - cx))
    div_y = cy * difference(far_y, near_y, u, ahead_y, 0.5 * (1.0 - cy))
    moved = u - fluid[...] * (div_x + div_y)
    moved_ref[...] = moved
    m_high, m_low = split(moved)
    b_high, b_low = split(basis[...])
    both = dot(b_high, jnp.concatenate([m_high, m_low], axis=1))
    term = both[:, :cells] + both[:, cells:] + dot(b_low, m_high)

    @pl.when(i == 0)
    def _():
        mom_ref[...] = term

    @pl.when(i > 0)
    def _():
        mom_ref[...] += term


def transport(upper, owner, total, far, near, here, ahead, basis, table, fluid):
    half, cells = here.shape
    count = half // BLOCK
    modes = basis.shape[0]
    offset = count if upper else 0
    block = pl.BlockSpec((BLOCK, cells), lambda i, s: (i, 0))
    if upper:
        sign = lambda i, s: ((i + 1) % 2, 0, 0)
    else:
        sign = lambda i, s: (i % 2, 0, 0)
    return pl.pallas_call(
        functools.partial(transport_kernel, upper, half, total),
        grid_spec=pltpu.PrefetchScalarGridSpec(
            num_scalar_prefetch=1,
            grid=(count,),
            in_specs=[
                block,
                block,
                block,
                block,
                pl.BlockSpec((modes, BLOCK), lambda i, s: (0, i + offset)),
                pl.BlockSpec((1, 2 * cells, 3 * cells), sign),
                pl.BlockSpec((1, cells), lambda i, s: (0, 0)),
            ],
            out_specs=[block, pl.BlockSpec((modes, cells), lambda i, s: (0, 0))],
        ),
        out_shape=[
            jax.ShapeDtypeStruct((half, cells), jnp.float32),
            jax.ShapeDtypeStruct((modes, cells), jnp.float32),
        ],
        cost_estimate=pl.CostEstimate(
            flops=2 * half * cells * (3 * modes + 6 * cells),
            bytes_accessed=4 * half * (5 * cells + modes),
            transcendentals=0,
        ),
        name="transport",
    )(owner, far, near, here, ahead, basis, table, fluid)


def gain_of(basis_t, c_both, c_high):
    b_high, b_low = split(basis_t)
    cells = c_high.shape[1]
    both = dot(b_high, c_both)
    return both[:, :cells] + both[:, cells:] + dot(b_low, c_high)


def relax_kernel(blocks, moved_low, moved_up, basis, coll, fluid, out_ref):
    moved = jnp.where(pl.program_id(0) < blocks, moved_low[...], moved_up[...])
    c_high, c_low = split(coll[...])
    gain = gain_of(basis[...], jnp.concatenate([c_high, c_low], axis=1), c_high)
    out_ref[...] = moved + HALF_STEP * fluid[...] * gain


def relax(low, up, basis_t, coll, fluid):
    half, cells = low.shape
    modes = basis_t.shape[1]
    blocks = half // BLOCK
    return pl.pallas_call(
        functools.partial(relax_kernel, blocks),
        grid=(2 * blocks,),
        in_specs=[
            pl.BlockSpec((BLOCK, cells), lambda i: (jnp.minimum(i, blocks - 1), 0)),
            pl.BlockSpec((BLOCK, cells), lambda i: (jnp.maximum(i - blocks, 0), 0)),
            pl.BlockSpec((BLOCK, modes), lambda i: (i, 0)),
            pl.BlockSpec((modes, cells), lambda i: (0, 0)),
            pl.BlockSpec((1, cells), lambda i: (0, 0)),
        ],
        out_specs=pl.BlockSpec((BLOCK, cells), lambda i: (i, 0)),
        out_shape=jax.ShapeDtypeStruct((2 * half, cells), jnp.float32),
        cost_estimate=pl.CostEstimate(
            flops=12 * half * cells * modes,
            bytes_accessed=8 * half * (2 * cells + modes),
            transcendentals=0,
        ),
        name="relax",
    )(low, up, basis_t, coll, fluid)


def finish_kernel(blocks, width, *refs):
    done = refs[: width - 1]
    moved_low, moved_up, basis, coll, fluid, out_ref = refs[width - 1 :]
    moved = jnp.where(pl.program_id(0) < blocks, moved_low[...], moved_up[...])
    c_high, c_low = split(coll[...])
    gain = gain_of(basis[...], jnp.concatenate([c_high, c_low], axis=1), c_high)
    rows = moved.shape[0]
    for x in range(width - 1):
        out_ref[pl.ds(x, rows, stride=width), :] = done[x][...]
    out_ref[pl.ds(width - 1, rows, stride=width), :] = moved + HALF_STEP * fluid[...] * gain


def finish(done, low, up, basis_t, coll, fluid):
    half, cells = low.shape
    modes = basis_t.shape[1]
    width = len(done) + 1
    blocks = half // BLOCK
    column = pl.BlockSpec((BLOCK, cells), lambda i: (i, 0))
    return pl.pallas_call(
        functools.partial(finish_kernel, blocks, width),
        grid=(2 * blocks,),
        in_specs=[column] * (width - 1)
        + [
            pl.BlockSpec((BLOCK, cells), lambda i: (jnp.minimum(i, blocks - 1), 0)),
            pl.BlockSpec((BLOCK, cells), lambda i: (jnp.maximum(i - blocks, 0), 0)),
            pl.BlockSpec((BLOCK, modes), lambda i: (i, 0)),
            pl.BlockSpec((modes, cells), lambda i: (0, 0)),
            pl.BlockSpec((1, cells), lambda i: (0, 0)),
        ],
        out_specs=pl.BlockSpec((BLOCK * width, cells), lambda i: (i, 0)),
        out_shape=jax.ShapeDtypeStruct((2 * half * width, cells), jnp.float32),
        cost_estimate=pl.CostEstimate(
            flops=12 * half * cells * modes,
            bytes_accessed=8 * half * (2 * width * cells + modes),
            transcendentals=0,
        ),
        name="finish",
    )(*done, low, up, basis_t, coll, fluid)


def tables(following, preceding):
    rows = jnp.arange(following.shape[0], dtype=jnp.int32)

    def one_hot(index):
        return (rows[:, None] == index[None, :]).astype(jnp.bfloat16)

    def twice(index):
        table = one_hot(index)
        return jnp.dot(table, table)

    negative = jnp.concatenate([one_hot(following), twice(following), one_hot(preceding)], axis=1)
    positive = jnp.concatenate([one_hot(preceding), twice(preceding), one_hot(following)], axis=1)
    both = jnp.stack([negative, positive])
    return jnp.concatenate([both, both], axis=1)


def matmul(left, right):
    a_high, a_low = split(left)
    b_high, b_low = split(right)
    return dot(a_high, b_high) + dot(a_high, b_low) + dot(a_low, b_high)


def collide_kernel(n, part_ref, left_ref, right_ref, mixing_ref, out_ref, share, moments, landed, send, recv):
    me = lax.axis_index("vel")
    rows = part_ref.shape[0] // n
    own = pl.ds(pl.multiple_of(me * rows, rows), rows)
    peers = [lax.rem(me + k, n) for k in range(1, n)]

    barrier = pltpu.get_barrier_semaphore()
    for peer in peers:
        pl.semaphore_signal(
            barrier, inc=1, device_id={"vel": peer}, device_id_type=pl.DeviceIdType.MESH
        )
    pl.semaphore_wait(barrier, n - 1)

    def total(phase, source, target):
        def copies(step, piece):
            made = []
            for k, peer in enumerate(peers):
                from_ref, to_ref = piece(k, peer)
                made.append(
                    pltpu.make_async_remote_copy(
                        src_ref=from_ref,
                        dst_ref=to_ref,
                        send_sem=send.at[phase + step, k],
                        recv_sem=recv.at[phase + step, k],
                        device_id={"vel": peer},
                        device_id_type=pl.DeviceIdType.MESH,
                    )
                )
            for copy in made:
                copy.start()
            for copy in made:
                copy.wait()

        copies(
            0,
            lambda k, peer: (
                source.at[pl.ds(pl.multiple_of(peer * rows, rows), rows)],
                landed.at[phase // 2, k],
            ),
        )
        added = source[own, :]
        for k in range(n - 1):
            added = added + landed[phase // 2, k]
        target[own, :] = added
        copies(1, lambda k, peer: (target.at[own], target.at[own]))

    total(0, part_ref, moments)
    value = moments[...]
    product = matmul(left_ref[...], value) * matmul(right_ref[...], value)
    share[...] = matmul(mixing_ref[...], product)
    total(2, share, out_ref)


def collide(part, left, right, mixing):
    n = lax.axis_size("vel")
    modes, cells = part.shape
    f32 = jnp.float32
    return pl.pallas_call(
        functools.partial(collide_kernel, n),
        in_specs=[pl.BlockSpec(memory_space=pltpu.VMEM)] * 4,
        out_specs=pl.BlockSpec(memory_space=pltpu.VMEM),
        out_shape=jax.ShapeDtypeStruct((modes, cells), f32),
        scratch_shapes=[
            pltpu.VMEM((modes, cells), f32),
            pltpu.VMEM((modes, cells), f32),
            pltpu.VMEM((2, n - 1, modes // n, cells), f32),
            pltpu.SemaphoreType.DMA((4, n - 1)),
            pltpu.SemaphoreType.DMA((4, n - 1)),
        ],
        compiler_params=pltpu.CompilerParams(
            collective_id=0, has_side_effects=True, vmem_limit_bytes=24 << 20
        ),
        cost_estimate=pl.CostEstimate(
            flops=40 * modes * cells * modes, bytes_accessed=16 * modes * modes, transcendentals=0
        ),
        name="collide",
    )(part, left, right, mixing)


def on_device(dist, basis, left_factor, right_factor, mixing, next_cell, prev_cell, cell_kind):
    per_device, width, extent_y = dist.shape
    half = per_device // 2
    total = per_device * lax.axis_size("vel")
    owner = jnp.reshape(lax.axis_index("vel"), (1,)).astype(jnp.int32)
    fluid = (1 - cell_kind).astype(jnp.float32)
    last = width - 1

    low, up = {}, {}
    plan = [
        (up, last, -1, 1),
        (low, 0, width, -1),
        (up, last - 1, -2, 1),
        (low, last, -1, 1),
        (low, 1, width + 1, -1),
        (up, 0, width, -1),
    ]
    landed = []
    for side, x, to, by in plan:
        side[x] = dist[half:, x] if side is up else dist[:half, x]
        sent = side[x]
        if len(landed) >= IN_FLIGHT:
            sent, _ = lax.optimization_barrier((sent, landed[-IN_FLIGHT]))
        side[to] = shifted(sent, by)
        landed.append(side[to])
    for x in range(width):
        if x not in low:
            low[x] = dist[:half, x]
        if x not in up:
            up[x] = dist[half:, x]

    basis_t = basis.T
    order = list(range(1, last)) + [0, last]
    moved, collision, done = {}, {}, {}
    for x in order:
        table = tables(next_cell[x], prev_cell[x])
        row = fluid[x : x + 1]
        m_low, s_low = transport(
            False, owner, total, low[x + 2], low[x + 1], low[x], low[x - 1], basis, table, row
        )
        ahead = up[x + 1]
        if x == last:
            held = lax.optimization_barrier((ahead, m_low, *(done[y] for y in range(last))))
            ahead, m_low = held[:2]
            done = dict(enumerate(held[2:]))
        m_up, s_up = transport(
            True, owner, total, up[x - 2], up[x - 1], up[x], ahead, basis, table, row
        )
        moved[x] = (m_low, m_up)
        part = s_low + s_up
        if x != order[0]:
            part, _ = lax.optimization_barrier((part, collision[before]))
        collision[x] = collide(part, left_factor, right_factor, mixing)
        before = x
        if x != last:
            done[x] = relax(*moved[x], basis_t, collision[x], row)

    done = [done[x] for x in range(last)]
    out = finish(done, *moved[last], basis_t, collision[last], fluid[last:])
    return out.reshape(dist.shape)


def solution(mesh):
    in_specs = (
        P("vel", "cells", None),
        P(None, "vel"),
        P("vel", None),
        P("vel", None),
        P(None, "vel"),
        P("cells", None),
        P("cells", None),
        P("cells", None),
    )
    out_specs = P("vel", "cells", None)
    return jax.shard_map(
        on_device, mesh=mesh, in_specs=in_specs, out_specs=out_specs, check_vma=False
    )
```

```python
import functools

import jax
import jax.numpy as jnp
from jax import lax
from jax.experimental import pallas as pl
from jax.experimental.pallas import tpu as pltpu
from jax.sharding import PartitionSpec as P

NV1 = 32
SPEED_RANGE = 6.4
RATIO_X = 0.2
RATIO_Y = 0.12
HALF_STEP = 0.5
IN_FLIGHT = 2
BLOCK = NV1 * NV1 // 2


def shifted(x, by):
    size = lax.axis_size("cells")
    return lax.ppermute(x, "cells", [(i, (i + by) % size) for i in range(size)])


def minmod(a, b):
    return jnp.maximum(jnp.minimum(a, b), 0.0) + jnp.minimum(jnp.maximum(a, b), 0.0)


def split(x):
    high = x.astype(jnp.bfloat16)
    low = (x - high.astype(jnp.float32)).astype(jnp.bfloat16)
    return high, low


def dot(a, b):
    return jnp.dot(a, b, preferred_element_type=jnp.float32)


def difference(far, near, here, ahead, factor):
    step = here - near
    return (here + factor * minmod(step, ahead - here)) - (
        near + factor * minmod(near - far, step)
    )


def transport_kernel(upper, half, total, owner_ref, far, near, here, ahead, b_high, b_low, table, fluid, moved_ref, mom_ref):
    i = pl.program_id(0)
    start = owner_ref[0] * half + i * BLOCK
    points = NV1
    middle = (points - 1) * 0.5
    step = SPEED_RANGE / points
    rows = lax.broadcasted_iota(jnp.int32, here.shape, 0) // points
    if upper:
        first = total - 1 - start
        index_y = (first // points) % points - rows
    else:
        first = start
        index_y = (first // points) % points + rows
    index_x = first // (points * points)
    cx = jnp.abs((index_x.astype(jnp.float32) - middle) * step * RATIO_X)
    cy = jnp.abs((index_y.astype(jnp.float32) - middle) * (step * RATIO_Y))
    u = here[...]
    high, low = split(u)
    picked = dot(jnp.concatenate([high, low], axis=1), table[0])
    cells = u.shape[1]
    near_y = picked[:, :cells]
    far_y = picked[:, cells : 2 * cells]
    ahead_y = picked[:, 2 * cells :]
    div_x = cx * difference(far[...], near[...], u, ahead[...], 0.5 * (1.0 - cx))
    div_y = cy * difference(far_y, near_y, u, ahead_y, 0.5 * (1.0 - cy))
    moved = u - fluid[...] * (div_x + div_y)
    moved_ref[...] = moved
    m_high, m_low = split(moved)
    both = dot(b_high[...], jnp.concatenate([m_high, m_low], axis=1))
    term = both[:, :cells] + both[:, cells:] + dot(b_low[...], m_high)

    @pl.when(i == 0)
    def _():
        mom_ref[...] = term

    @pl.when(i > 0)
    def _():
        mom_ref[...] += term


def transport(upper, owner, total, far, near, here, ahead, basis, table, fluid):
    half, cells = here.shape
    count = half // BLOCK
    modes = basis[0].shape[0]
    offset = count if upper else 0
    block = pl.BlockSpec((BLOCK, cells), lambda i, s: (i, 0))
    if upper:
        sign = lambda i, s: ((i + 1) % 2, 0, 0)
    else:
        sign = lambda i, s: (i % 2, 0, 0)
    return pl.pallas_call(
        functools.partial(transport_kernel, upper, half, total),
        grid_spec=pltpu.PrefetchScalarGridSpec(
            num_scalar_prefetch=1,
            grid=(count,),
            in_specs=[
                block,
                block,
                block,
                block,
                pl.BlockSpec((modes, BLOCK), lambda i, s: (0, i + offset)),
                pl.BlockSpec((modes, BLOCK), lambda i, s: (0, i + offset)),
                pl.BlockSpec((1, 2 * cells, 3 * cells), sign),
                pl.BlockSpec((1, cells), lambda i, s: (0, 0)),
            ],
            out_specs=[block, pl.BlockSpec((modes, cells), lambda i, s: (0, 0))],
        ),
        out_shape=[
            jax.ShapeDtypeStruct((half, cells), jnp.float32),
            jax.ShapeDtypeStruct((modes, cells), jnp.float32),
        ],
        cost_estimate=pl.CostEstimate(
            flops=2 * half * cells * (3 * modes + 6 * cells),
            bytes_accessed=4 * half * (5 * cells + modes),
            transcendentals=0,
        ),
        name="transport",
    )(owner, far, near, here, ahead, *basis, table, fluid)


def prepare_kernel(basis, high_ref, low_ref, turned_high_ref, turned_low_ref):
    value = basis[...]
    high_ref[...], low_ref[...] = split(value)
    turned_high_ref[...], turned_low_ref[...] = split(value.T)


def prepare(basis):
    modes, count = basis.shape
    flat = pl.BlockSpec((modes, BLOCK), lambda i: (0, i))
    turned = pl.BlockSpec((BLOCK, modes), lambda i: (i, 0))
    bf16 = jnp.bfloat16
    return pl.pallas_call(
        prepare_kernel,
        grid=(count // BLOCK,),
        in_specs=[flat],
        out_specs=[flat, flat, turned, turned],
        out_shape=[jax.ShapeDtypeStruct((modes, count), bf16)] * 2
        + [jax.ShapeDtypeStruct((count, modes), bf16)] * 2,
        cost_estimate=pl.CostEstimate(
            flops=modes * count, bytes_accessed=12 * modes * count, transcendentals=0
        ),
        name="prepare",
    )(basis)


def columns_kernel(width, field, *outs):
    rows = outs[0].shape[0]
    for x in range(width):
        outs[x][...] = field[pl.ds(x, rows, stride=width), :]


def columns(field, width, half, upper):
    cells = field.shape[1]
    size = 2 * BLOCK if half % (2 * BLOCK) == 0 else BLOCK
    count = half // size
    offset = count if upper else 0
    return pl.pallas_call(
        functools.partial(columns_kernel, width),
        grid=(count,),
        in_specs=[pl.BlockSpec((size * width, cells), lambda i: (i + offset, 0))],
        out_specs=[pl.BlockSpec((size, cells), lambda i: (i, 0))] * width,
        out_shape=[jax.ShapeDtypeStruct((half, cells), jnp.float32)] * width,
        cost_estimate=pl.CostEstimate(
            flops=0, bytes_accessed=8 * half * width * cells, transcendentals=0
        ),
        name="columns",
    )(field)


def finish_kernel(blocks, width, *refs):
    lows, ups, colls = refs[:width], refs[width : 2 * width], refs[2 * width : 3 * width]
    b_high, b_low, fluid, out_ref, c_high, c_low = refs[3 * width :]
    i = pl.program_id(0)
    rows, cells = lows[0].shape

    @pl.when(i == 0)
    def _():
        for x in range(width):
            part = pl.ds(x * cells, cells)
            c_high[:, part], c_low[:, part] = split(colls[x][...])

    gain = (
        dot(b_high[...], c_high[...]) + dot(b_high[...], c_low[...]) + dot(b_low[...], c_high[...])
    )
    for x in range(width):
        moved = jnp.where(i < blocks, lows[x][...], ups[x][...])
        value = moved + HALF_STEP * fluid[x : x + 1, :] * gain[:, x * cells : (x + 1) * cells]
        out_ref[pl.ds(x, rows, stride=width), :] = value


def finish(lows, ups, colls, turned, fluid):
    half, cells = lows[0].shape
    modes = colls[0].shape[0]
    width = len(lows)
    blocks = half // BLOCK
    return pl.pallas_call(
        functools.partial(finish_kernel, blocks, width),
        grid=(2 * blocks,),
        in_specs=[pl.BlockSpec((BLOCK, cells), lambda i: (jnp.minimum(i, blocks - 1), 0))] * width
        + [pl.BlockSpec((BLOCK, cells), lambda i: (jnp.maximum(i - blocks, 0), 0))] * width
        + [pl.BlockSpec((modes, cells), lambda i: (0, 0))] * width
        + [pl.BlockSpec((BLOCK, modes), lambda i: (i, 0))] * 2
        + [pl.BlockSpec((width, cells), lambda i: (0, 0))],
        out_specs=pl.BlockSpec((BLOCK * width, cells), lambda i: (i, 0)),
        out_shape=jax.ShapeDtypeStruct((2 * half * width, cells), jnp.float32),
        scratch_shapes=[pltpu.VMEM((modes, width * cells), jnp.bfloat16)] * 2,
        cost_estimate=pl.CostEstimate(
            flops=12 * half * cells * modes * width,
            bytes_accessed=8 * half * (2 * width * cells + modes),
            transcendentals=0,
        ),
        name="finish",
    )(*lows, *ups, *colls, *turned, fluid)


def tables(following, preceding):
    rows = jnp.arange(following.shape[0], dtype=jnp.int32)

    def one_hot(index):
        return (rows[:, None] == index[None, :]).astype(jnp.bfloat16)

    def twice(index):
        table = one_hot(index)
        return jnp.dot(table, table)

    negative = jnp.concatenate([one_hot(following), twice(following), one_hot(preceding)], axis=1)
    positive = jnp.concatenate([one_hot(preceding), twice(preceding), one_hot(following)], axis=1)
    both = jnp.stack([negative, positive])
    return jnp.concatenate([both, both], axis=1)


def matmul(left, right):
    a_high, a_low = split(left)
    b_high, b_low = split(right)
    return dot(a_high, b_high) + dot(a_high, b_low) + dot(a_low, b_high)


def collide_kernel(n, part_ref, left_ref, right_ref, mixing_ref, out_ref, share, moments, landed, send, recv):
    me = lax.axis_index("vel")
    rows = part_ref.shape[0] // n
    own = pl.ds(pl.multiple_of(me * rows, rows), rows)
    peers = [lax.rem(me + k, n) for k in range(1, n)]

    barrier = pltpu.get_barrier_semaphore()
    for peer in peers:
        pl.semaphore_signal(
            barrier, inc=1, device_id={"vel": peer}, device_id_type=pl.DeviceIdType.MESH
        )
    pl.semaphore_wait(barrier, n - 1)

    def total(phase, source, target):
        def copies(step, piece):
            made = []
            for k, peer in enumerate(peers):
                from_ref, to_ref = piece(k, peer)
                made.append(
                    pltpu.make_async_remote_copy(
                        src_ref=from_ref,
                        dst_ref=to_ref,
                        send_sem=send.at[phase + step, k],
                        recv_sem=recv.at[phase + step, k],
                        device_id={"vel": peer},
                        device_id_type=pl.DeviceIdType.MESH,
                    )
                )
            for copy in made:
                copy.start()
            for copy in made:
                copy.wait()

        copies(
            0,
            lambda k, peer: (
                source.at[pl.ds(pl.multiple_of(peer * rows, rows), rows)],
                landed.at[phase // 2, k],
            ),
        )
        added = source[own, :]
        for k in range(n - 1):
            added = added + landed[phase // 2, k]
        target[own, :] = added
        copies(1, lambda k, peer: (target.at[own], target.at[own]))

    total(0, part_ref, moments)
    value = moments[...]
    product = matmul(left_ref[...], value) * matmul(right_ref[...], value)
    share[...] = matmul(mixing_ref[...], product)
    total(2, share, out_ref)


def collide(part, left, right, mixing):
    n = lax.axis_size("vel")
    modes, cells = part.shape
    f32 = jnp.float32
    return pl.pallas_call(
        functools.partial(collide_kernel, n),
        in_specs=[pl.BlockSpec(memory_space=pltpu.VMEM)] * 4,
        out_specs=pl.BlockSpec(memory_space=pltpu.VMEM),
        out_shape=jax.ShapeDtypeStruct((modes, cells), f32),
        scratch_shapes=[
            pltpu.VMEM((modes, cells), f32),
            pltpu.VMEM((modes, cells), f32),
            pltpu.VMEM((2, n - 1, modes // n, cells), f32),
            pltpu.SemaphoreType.DMA((4, n - 1)),
            pltpu.SemaphoreType.DMA((4, n - 1)),
        ],
        compiler_params=pltpu.CompilerParams(
            collective_id=0, has_side_effects=True, vmem_limit_bytes=24 << 20
        ),
        cost_estimate=pl.CostEstimate(
            flops=40 * modes * cells * modes, bytes_accessed=16 * modes * modes, transcendentals=0
        ),
        name="collide",
    )(part, left, right, mixing)


def on_device(dist, basis, left_factor, right_factor, mixing, next_cell, prev_cell, cell_kind):
    per_device, width, extent_y = dist.shape
    half = per_device // 2
    total = per_device * lax.axis_size("vel")
    owner = jnp.reshape(lax.axis_index("vel"), (1,)).astype(jnp.int32)
    fluid = (1 - cell_kind).astype(jnp.float32)
    last = width - 1

    field = dist.reshape(per_device * width, extent_y)
    up = dict(enumerate(columns(field, width, half, True)))
    field, up[0] = lax.optimization_barrier((field, up[0]))
    low = dict(enumerate(columns(field, width, half, False)))
    split_basis = prepare(basis)
    turned = split_basis[2:]
    split_basis = split_basis[:2]
    table = [tables(next_cell[x], prev_cell[x]) for x in range(width)]

    plan = [
        (up, last, -1, 1),
        (low, 0, width, -1),
        (up, last - 1, -2, 1),
        (low, last, -1, 1),
        (low, 1, width + 1, -1),
        (up, 0, width, -1),
    ]
    order = list(range(1, last)) + [0, last]
    waiting = [(upper, x) for upper in (False, True) for x in order]
    moved, sums, collision = {}, {}, {}
    token = owner

    def held(value):
        return lax.optimization_barrier((value, token))[0]

    def send(i, after=None):
        side, x, to, by = plan[i]
        sent = side[x] if after is None else lax.optimization_barrier((side[x], after))[0]
        return shifted(sent, by)

    flying = [send(i) for i in range(IN_FLIGHT)]
    for i in range(len(plan) + 1):
        if i > 0:
            side, x, to, by = plan[i - 1]
            side[to] = held(flying[i - 1])
            if len(flying) < len(plan):
                flying.append(send(len(flying), side[to]))
        for upper, x in list(waiting):
            side = up if upper else low
            needs = (x - 2, x - 1, x, x + 1) if upper else (x + 2, x + 1, x, x - 1)
            if any(need not in side for need in needs):
                continue
            waiting.remove((upper, x))
            moved[upper, x], part = transport(
                upper,
                held(owner),
                total,
                *(side[need] for need in needs),
                split_basis,
                table[x],
                fluid[x : x + 1],
            )
            token = part
            if x not in sums:
                sums[x] = part
                continue
            part = held(sums[x] + part)
            collision[x] = collide(part, left_factor, right_factor, mixing)
            token = collision[x]

    out = finish(
        [moved[False, x] for x in range(width)],
        [moved[True, x] for x in range(width)],
        [collision[x] for x in range(width)],
        turned,
        fluid,
    )
    return out.reshape(dist.shape)


def solution(mesh):
    in_specs = (
        P("vel", "cells", None),
        P(None, "vel"),
        P("vel", None),
        P("vel", None),
        P(None, "vel"),
        P("cells", None),
        P("cells", None),
        P("cells", None),
    )
    out_specs = P("vel", "cells", None)
    return jax.shard_map(
        on_device, mesh=mesh, in_specs=in_specs, out_specs=out_specs, check_vma=False
    )
```

```python
import functools

import jax
import jax.numpy as jnp
from jax import lax
from jax.experimental import pallas as pl
from jax.experimental.pallas import tpu as pltpu
from jax.sharding import PartitionSpec as P

NV1 = 32
SPEED_RANGE = 6.4
RATIO_X = 0.2
RATIO_Y = 0.12
HALF_STEP = 0.5
LAST_PIECES = 2
BLOCK = NV1 * NV1 // 2


def shifted(x, by):
    size = lax.axis_size("cells")
    return lax.ppermute(x, "cells", [(i, (i + by) % size) for i in range(size)])


def minmod(a, b):
    return jnp.maximum(jnp.minimum(a, b), 0.0) + jnp.minimum(jnp.maximum(a, b), 0.0)


def split(x):
    high = x.astype(jnp.bfloat16)
    low = (x - high.astype(jnp.float32)).astype(jnp.bfloat16)
    return high, low


def dot(a, b):
    return jnp.dot(a, b, preferred_element_type=jnp.float32)


def difference(far, near, here, ahead, factor):
    step = here - near
    return (here + factor * minmod(step, ahead - here)) - (
        near + factor * minmod(near - far, step)
    )


def transport_kernel(upper, half, total, first_block, owner_ref, far, near, here, ahead, b_high, b_low, table, fluid, *rest):
    moved_ref, mom_ref = rest[-2:]
    i = pl.program_id(0)
    start = owner_ref[0] * half + (i + first_block) * BLOCK
    points = NV1
    middle = (points - 1) * 0.5
    step = SPEED_RANGE / points
    rows = lax.broadcasted_iota(jnp.int32, here.shape, 0) // points
    if upper:
        first = total - 1 - start
        index_y = (first // points) % points - rows
    else:
        first = start
        index_y = (first // points) % points + rows
    index_x = first // (points * points)
    cx = jnp.abs((index_x.astype(jnp.float32) - middle) * step * RATIO_X)
    cy = jnp.abs((index_y.astype(jnp.float32) - middle) * (step * RATIO_Y))
    u = here[...]
    high, low = split(u)
    picked = dot(jnp.concatenate([high, low], axis=1), table[0])
    cells = u.shape[1]
    near_y = picked[:, :cells]
    far_y = picked[:, cells : 2 * cells]
    ahead_y = picked[:, 2 * cells :]
    div_x = cx * difference(far[...], near[...], u, ahead[...], 0.5 * (1.0 - cx))
    div_y = cy * difference(far_y, near_y, u, ahead_y, 0.5 * (1.0 - cy))
    moved = u - fluid[...] * (div_x + div_y)
    moved_ref[...] = moved
    m_high, m_low = split(moved)
    both = dot(b_high[...], jnp.concatenate([m_high, m_low], axis=1))
    term = both[:, :cells] + both[:, cells:] + dot(b_low[...], m_high)

    @pl.when(i == 0)
    def _():
        mom_ref[...] = term if len(rest) == 2 else rest[0][...] + term

    @pl.when(i > 0)
    def _():
        mom_ref[...] += term


def transport(upper, owner, total, far, near, here, ahead, basis, table, fluid, first=0, before=()):
    half, cells = here.shape
    count = ahead.shape[0] // BLOCK
    modes = basis[0].shape[0]
    offset = half // BLOCK if upper else 0
    flip = first + 1 if upper else first
    block = pl.BlockSpec((BLOCK, cells), lambda i, s: (i + first, 0))
    sums = pl.BlockSpec((modes, cells), lambda i, s: (0, 0))
    return pl.pallas_call(
        functools.partial(transport_kernel, upper, half, total, first),
        grid_spec=pltpu.PrefetchScalarGridSpec(
            num_scalar_prefetch=1,
            grid=(count,),
            in_specs=[
                block,
                block,
                block,
                pl.BlockSpec((BLOCK, cells), lambda i, s: (i, 0)),
                pl.BlockSpec((modes, BLOCK), lambda i, s: (0, i + first + offset)),
                pl.BlockSpec((modes, BLOCK), lambda i, s: (0, i + first + offset)),
                pl.BlockSpec((1, 2 * cells, 3 * cells), lambda i, s: ((i + flip) % 2, 0, 0)),
                pl.BlockSpec((1, cells), lambda i, s: (0, 0)),
                *([sums, pl.BlockSpec(memory_space=pl.ANY)] if before else []),
            ],
            out_specs=[block, sums],
        ),
        out_shape=[
            jax.ShapeDtypeStruct((half, cells), jnp.float32),
            jax.ShapeDtypeStruct((modes, cells), jnp.float32),
        ],
        input_output_aliases={10: 0} if before else {},
        cost_estimate=pl.CostEstimate(
            flops=2 * count * BLOCK * cells * (3 * modes + 6 * cells),
            bytes_accessed=4 * count * BLOCK * (5 * cells + modes),
            transcendentals=0,
        ),
        name="transport",
    )(owner, far, near, here, ahead, *basis, table, fluid, *before)


def prepare_kernel(basis, high_ref, low_ref, turned_high_ref, turned_low_ref):
    value = basis[...]
    high_ref[...], low_ref[...] = split(value)
    turned_high_ref[...], turned_low_ref[...] = split(value.T)


def prepare(basis):
    modes, count = basis.shape
    flat = pl.BlockSpec((modes, BLOCK), lambda i: (0, i))
    turned = pl.BlockSpec((BLOCK, modes), lambda i: (i, 0))
    bf16 = jnp.bfloat16
    return pl.pallas_call(
        prepare_kernel,
        grid=(count // BLOCK,),
        in_specs=[flat],
        out_specs=[flat, flat, turned, turned],
        out_shape=[jax.ShapeDtypeStruct((modes, count), bf16)] * 2
        + [jax.ShapeDtypeStruct((count, modes), bf16)] * 2,
        cost_estimate=pl.CostEstimate(
            flops=modes * count, bytes_accessed=12 * modes * count, transcendentals=0
        ),
        name="prepare",
    )(basis)


def columns_kernel(width, field, *outs):
    rows = outs[0].shape[0]
    for x in range(width):
        outs[x][...] = field[pl.ds(x, rows, stride=width), :]


def columns(field, width, half, upper):
    cells = field.shape[1]
    size = 2 * BLOCK if half % (2 * BLOCK) == 0 else BLOCK
    count = half // size
    offset = count if upper else 0
    return pl.pallas_call(
        functools.partial(columns_kernel, width),
        grid=(count,),
        in_specs=[pl.BlockSpec((size * width, cells), lambda i: (i + offset, 0))],
        out_specs=[pl.BlockSpec((size, cells), lambda i: (i, 0))] * width,
        out_shape=[jax.ShapeDtypeStruct((half, cells), jnp.float32)] * width,
        cost_estimate=pl.CostEstimate(
            flops=0, bytes_accessed=8 * half * width * cells, transcendentals=0
        ),
        name="columns",
    )(field)


def finish_kernel(blocks, width, *refs):
    lows, ups, colls = refs[:width], refs[width : 2 * width], refs[2 * width : 3 * width]
    b_high, b_low, fluid, out_ref, c_high, c_low = refs[3 * width :]
    i = pl.program_id(0)
    rows, cells = lows[0].shape

    @pl.when(i == 0)
    def _():
        for x in range(width):
            part = pl.ds(x * cells, cells)
            c_high[:, part], c_low[:, part] = split(colls[x][...])

    gain = (
        dot(b_high[...], c_high[...]) + dot(b_high[...], c_low[...]) + dot(b_low[...], c_high[...])
    )
    for x in range(width):
        moved = jnp.where(i < blocks, lows[x][...], ups[x][...])
        value = moved + HALF_STEP * fluid[x : x + 1, :] * gain[:, x * cells : (x + 1) * cells]
        out_ref[pl.ds(x, rows, stride=width), :] = value


def finish(lows, ups, colls, turned, fluid):
    half, cells = lows[0].shape
    modes = colls[0].shape[0]
    width = len(lows)
    size = 2 * BLOCK if half % (2 * BLOCK) == 0 else BLOCK
    blocks = half // size
    return pl.pallas_call(
        functools.partial(finish_kernel, blocks, width),
        grid=(2 * blocks,),
        in_specs=[pl.BlockSpec((size, cells), lambda i: (jnp.minimum(i, blocks - 1), 0))] * width
        + [pl.BlockSpec((size, cells), lambda i: (jnp.maximum(i - blocks, 0), 0))] * width
        + [pl.BlockSpec((modes, cells), lambda i: (0, 0))] * width
        + [pl.BlockSpec((size, modes), lambda i: (i, 0))] * 2
        + [pl.BlockSpec((width, cells), lambda i: (0, 0))],
        out_specs=pl.BlockSpec((size * width, cells), lambda i: (i, 0)),
        out_shape=jax.ShapeDtypeStruct((2 * half * width, cells), jnp.float32),
        scratch_shapes=[pltpu.VMEM((modes, width * cells), jnp.bfloat16)] * 2,
        cost_estimate=pl.CostEstimate(
            flops=12 * half * cells * modes * width,
            bytes_accessed=8 * half * (2 * width * cells + modes),
            transcendentals=0,
        ),
        name="finish",
    )(*lows, *ups, *colls, *turned, fluid)


def tables(following, preceding):
    rows = jnp.arange(following.shape[0], dtype=jnp.int32)

    def one_hot(index):
        return (rows[:, None] == index[None, :]).astype(jnp.bfloat16)

    def twice(index):
        table = one_hot(index)
        return jnp.dot(table, table)

    negative = jnp.concatenate([one_hot(following), twice(following), one_hot(preceding)], axis=1)
    positive = jnp.concatenate([one_hot(preceding), twice(preceding), one_hot(following)], axis=1)
    both = jnp.stack([negative, positive])
    return jnp.concatenate([both, both], axis=1)


def matmul(left, right):
    a_high, a_low = split(left)
    b_high, b_low = split(right)
    return dot(a_high, b_high) + dot(a_high, b_low) + dot(a_low, b_high)


def collide_kernel(n, part_ref, left_ref, right_ref, mixing_ref, out_ref, share, moments, landed, send, recv):
    me = lax.axis_index("vel")
    rows = part_ref.shape[0] // n
    own = pl.ds(pl.multiple_of(me * rows, rows), rows)
    peers = [lax.rem(me + k, n) for k in range(1, n)]

    barrier = pltpu.get_barrier_semaphore()
    for peer in peers:
        pl.semaphore_signal(
            barrier, inc=1, device_id={"vel": peer}, device_id_type=pl.DeviceIdType.MESH
        )
    pl.semaphore_wait(barrier, n - 1)

    def total(phase, source, target):
        def copies(step, piece):
            made = []
            for k, peer in enumerate(peers):
                from_ref, to_ref = piece(k, peer)
                made.append(
                    pltpu.make_async_remote_copy(
                        src_ref=from_ref,
                        dst_ref=to_ref,
                        send_sem=send.at[phase + step, k],
                        recv_sem=recv.at[phase + step, k],
                        device_id={"vel": peer},
                        device_id_type=pl.DeviceIdType.MESH,
                    )
                )
            for copy in made:
                copy.start()
            for copy in made:
                copy.wait()

        copies(
            0,
            lambda k, peer: (
                source.at[pl.ds(pl.multiple_of(peer * rows, rows), rows)],
                landed.at[phase // 2, k],
            ),
        )
        added = source[own, :]
        for k in range(n - 1):
            added = added + landed[phase // 2, k]
        target[own, :] = added
        copies(1, lambda k, peer: (target.at[own], target.at[own]))

    total(0, part_ref, moments)
    value = moments[...]
    product = matmul(left_ref[...], value) * matmul(right_ref[...], value)
    share[...] = matmul(mixing_ref[...], product)
    total(2, share, out_ref)


def collide(part, left, right, mixing):
    n = lax.axis_size("vel")
    modes, cells = part.shape
    f32 = jnp.float32
    return pl.pallas_call(
        functools.partial(collide_kernel, n),
        in_specs=[pl.BlockSpec(memory_space=pltpu.VMEM)] * 4,
        out_specs=pl.BlockSpec(memory_space=pltpu.VMEM),
        out_shape=jax.ShapeDtypeStruct((modes, cells), f32),
        scratch_shapes=[
            pltpu.VMEM((modes, cells), f32),
            pltpu.VMEM((modes, cells), f32),
            pltpu.VMEM((2, n - 1, modes // n, cells), f32),
            pltpu.SemaphoreType.DMA((4, n - 1)),
            pltpu.SemaphoreType.DMA((4, n - 1)),
        ],
        compiler_params=pltpu.CompilerParams(
            collective_id=0, has_side_effects=True, vmem_limit_bytes=24 << 20
        ),
        cost_estimate=pl.CostEstimate(
            flops=40 * modes * cells * modes, bytes_accessed=16 * modes * modes, transcendentals=0
        ),
        name="collide",
    )(part, left, right, mixing)


def on_device(dist, basis, left_factor, right_factor, mixing, next_cell, prev_cell, cell_kind):
    per_device, width, extent_y = dist.shape
    half = per_device // 2
    total = per_device * lax.axis_size("vel")
    owner = jnp.reshape(lax.axis_index("vel"), (1,)).astype(jnp.int32)
    fluid = (1 - cell_kind).astype(jnp.float32)
    last = width - 1

    field = dist.reshape(per_device * width, extent_y)
    up = dict(enumerate(columns(field, width, half, True)))
    field, up[0] = lax.optimization_barrier((field, up[0]))
    low = dict(enumerate(columns(field, width, half, False)))
    split_basis = prepare(basis)
    turned = split_basis[2:]
    split_basis = split_basis[:2]
    table = [tables(next_cell[x], prev_cell[x]) for x in range(width)]

    plan = [
        (up, last, -1, 1),
        (low, 0, width, -1),
        (up, last - 1, -2, 1),
        (low, last, -1, 1),
        (low, 1, width + 1, -1),
    ]
    piece = max(half // LAST_PIECES // BLOCK, 1) * BLOCK
    pieces = range(0, half, piece)
    order = list(range(1, last)) + [0, last]
    waiting = [(upper, x) for upper in (False, True) for x in order]
    moved, sums, collision = {}, {}, {}
    token = owner

    def held(value):
        return lax.optimization_barrier((value, token))[0]

    def send(i, after=None):
        if i < len(plan):
            side, x, to, by = plan[i]
            sent = side[x]
        else:
            start = pieces[i - len(plan)]
            sent, by = up[0][start : start + piece], -1
        if after is not None:
            sent = lax.optimization_barrier((sent, after))[0]
        return shifted(sent, by)

    def step(upper, x, *columns, **more):
        return transport(
            upper, held(owner), total, *columns, split_basis, table[x], fluid[x : x + 1], **more
        )

    count = len(plan) + len(pieces)
    flying = [send(0), send(1, split_basis[0])]
    for i in range(count + 1):
        if i > 0:
            landed = held(flying[i - 1])
            if len(flying) < count:
                flying.append(send(len(flying), landed))
            if i <= len(plan):
                side, x, to, by = plan[i - 1]
                side[to] = landed
            else:
                start = pieces[i - 1 - len(plan)]
                before = (token, moved[True, last]) if start else ()
                moved[True, last], token = step(
                    True,
                    last,
                    *(up[last - k] for k in (2, 1, 0)),
                    landed,
                    first=start // BLOCK,
                    before=before,
                )
        for upper, x in list(waiting):
            side = up if upper else low
            needs = (x - 2, x - 1, x, x + 1) if upper else (x + 2, x + 1, x, x - 1)
            if any(need not in side for need in needs):
                continue
            waiting.remove((upper, x))
            moved[upper, x], part = step(upper, x, *(side[need] for need in needs))
            token = part
            if x not in sums:
                sums[x] = part
                continue
            collision[x] = collide(held(sums[x] + part), left_factor, right_factor, mixing)
            token = collision[x]
    collision[last] = collide(sums[last] + token, left_factor, right_factor, mixing)

    out = finish(
        [moved[False, x] for x in range(width)],
        [moved[True, x] for x in range(width)],
        [collision[x] for x in range(width)],
        turned,
        fluid,
    )
    return out.reshape(dist.shape)


def solution(mesh):
    in_specs = (
        P("vel", "cells", None),
        P(None, "vel"),
        P("vel", None),
        P("vel", None),
        P(None, "vel"),
        P("cells", None),
        P("cells", None),
        P("cells", None),
    )
    out_specs = P("vel", "cells", None)
    return jax.shard_map(
        on_device, mesh=mesh, in_specs=in_specs, out_specs=out_specs, check_vma=False
    )
```

```python
import functools

import jax
import jax.numpy as jnp
from jax import lax
from jax.experimental import pallas as pl
from jax.experimental.pallas import tpu as pltpu
from jax.sharding import PartitionSpec as P

NV1 = 32
SPEED_RANGE = 6.4
RATIO_X = 0.2
RATIO_Y = 0.12
HALF_STEP = 0.5
LAST_PIECES = 2
BLOCK = NV1 * NV1 // 2


def shifted(x, by):
    size = lax.axis_size("cells")
    return lax.ppermute(x, "cells", [(i, (i + by) % size) for i in range(size)])


def minmod(a, b):
    return jnp.maximum(jnp.minimum(a, b), 0.0) + jnp.minimum(jnp.maximum(a, b), 0.0)


def split(x):
    high = x.astype(jnp.bfloat16)
    low = (x - high.astype(jnp.float32)).astype(jnp.bfloat16)
    return high, low


def dot(a, b):
    return jnp.dot(a, b, preferred_element_type=jnp.float32)


def difference(far, near, here, ahead, factor):
    step = here - near
    return (here + factor * minmod(step, ahead - here)) - (
        near + factor * minmod(near - far, step)
    )


def transport_kernel(upper, half, total, first_block, owner_ref, far, near, here, ahead, b_high, b_low, table, fluid, *rest):
    moved_ref, mom_ref = rest[-2:]
    i = pl.program_id(0)
    start = owner_ref[0] * half + (i + first_block) * BLOCK
    points = NV1
    middle = (points - 1) * 0.5
    step = SPEED_RANGE / points
    rows = lax.broadcasted_iota(jnp.int32, here.shape, 0) // points
    if upper:
        first = total - 1 - start
        index_y = (first // points) % points - rows
    else:
        first = start
        index_y = (first // points) % points + rows
    index_x = first // (points * points)
    cx = jnp.abs((index_x.astype(jnp.float32) - middle) * step * RATIO_X)
    cy = jnp.abs((index_y.astype(jnp.float32) - middle) * (step * RATIO_Y))
    u = here[...]
    high, low = split(u)
    picked = dot(jnp.concatenate([high, low], axis=1), table[0])
    cells = u.shape[1]
    near_y = picked[:, :cells]
    far_y = picked[:, cells : 2 * cells]
    ahead_y = picked[:, 2 * cells :]
    div_x = cx * difference(far[...], near[...], u, ahead[...], 0.5 * (1.0 - cx))
    div_y = cy * difference(far_y, near_y, u, ahead_y, 0.5 * (1.0 - cy))
    moved = u - fluid[...] * (div_x + div_y)
    moved_ref[...] = moved
    m_high, m_low = split(moved)
    both = dot(b_high[...], jnp.concatenate([m_high, m_low], axis=1))
    term = both[:, :cells] + both[:, cells:] + dot(b_low[...], m_high)

    @pl.when(i == 0)
    def _():
        mom_ref[...] = term if len(rest) == 2 else rest[0][...] + term

    @pl.when(i > 0)
    def _():
        mom_ref[...] += term


def transport(upper, owner, total, far, near, here, ahead, basis, table, fluid, first=0, before=()):
    half, cells = here.shape
    count = ahead.shape[0] // BLOCK
    modes = basis[0].shape[0]
    offset = half // BLOCK if upper else 0
    flip = first + 1 if upper else first
    block = pl.BlockSpec((BLOCK, cells), lambda i, s: (i + first, 0))
    sums = pl.BlockSpec((modes, cells), lambda i, s: (0, 0))
    return pl.pallas_call(
        functools.partial(transport_kernel, upper, half, total, first),
        grid_spec=pltpu.PrefetchScalarGridSpec(
            num_scalar_prefetch=1,
            grid=(count,),
            in_specs=[
                block,
                block,
                block,
                pl.BlockSpec((BLOCK, cells), lambda i, s: (i, 0)),
                pl.BlockSpec((modes, BLOCK), lambda i, s: (0, i + first + offset)),
                pl.BlockSpec((modes, BLOCK), lambda i, s: (0, i + first + offset)),
                pl.BlockSpec((1, 2 * cells, 3 * cells), lambda i, s: ((i + flip) % 2, 0, 0)),
                pl.BlockSpec((1, cells), lambda i, s: (0, 0)),
                *([sums, pl.BlockSpec(memory_space=pl.ANY)] if before else []),
            ],
            out_specs=[block, sums],
        ),
        out_shape=[
            jax.ShapeDtypeStruct((half, cells), jnp.float32),
            jax.ShapeDtypeStruct((modes, cells), jnp.float32),
        ],
        input_output_aliases={10: 0} if before else {},
        cost_estimate=pl.CostEstimate(
            flops=2 * count * BLOCK * cells * (3 * modes + 6 * cells),
            bytes_accessed=4 * count * BLOCK * (5 * cells + modes),
            transcendentals=0,
        ),
        name="transport",
    )(owner, far, near, here, ahead, *basis, table, fluid, *before)


def prepare_kernel(basis, high_ref, low_ref, turned_high_ref, turned_low_ref):
    value = basis[...]
    high_ref[...], low_ref[...] = split(value)
    turned_high_ref[...], turned_low_ref[...] = split(value.T)


def prepare(basis):
    modes, count = basis.shape
    flat = pl.BlockSpec((modes, BLOCK), lambda i: (0, i))
    turned = pl.BlockSpec((BLOCK, modes), lambda i: (i, 0))
    bf16 = jnp.bfloat16
    return pl.pallas_call(
        prepare_kernel,
        grid=(count // BLOCK,),
        in_specs=[flat],
        out_specs=[flat, flat, turned, turned],
        out_shape=[jax.ShapeDtypeStruct((modes, count), bf16)] * 2
        + [jax.ShapeDtypeStruct((count, modes), bf16)] * 2,
        cost_estimate=pl.CostEstimate(
            flops=modes * count, bytes_accessed=12 * modes * count, transcendentals=0
        ),
        name="prepare",
    )(basis)


def columns_kernel(width, field, *outs):
    rows = outs[0].shape[0]
    for x in range(width):
        outs[x][...] = field[pl.ds(x, rows, stride=width), :]


def columns(field, width, half, upper):
    cells = field.shape[1]
    size = 2 * BLOCK if half % (2 * BLOCK) == 0 else BLOCK
    count = half // size
    offset = count if upper else 0
    return pl.pallas_call(
        functools.partial(columns_kernel, width),
        grid=(count,),
        in_specs=[pl.BlockSpec((size * width, cells), lambda i: (i + offset, 0))],
        out_specs=[pl.BlockSpec((size, cells), lambda i: (i, 0))] * width,
        out_shape=[jax.ShapeDtypeStruct((half, cells), jnp.float32)] * width,
        cost_estimate=pl.CostEstimate(
            flops=0, bytes_accessed=8 * half * width * cells, transcendentals=0
        ),
        name="columns",
    )(field)


def finish_kernel(blocks, width, *refs):
    lows, ups, colls = refs[:width], refs[width : 2 * width], refs[2 * width : 3 * width]
    b_high, b_low, fluid, out_ref, c_high, c_low = refs[3 * width :]
    i = pl.program_id(0)
    rows, cells = lows[0].shape

    @pl.when(i == 0)
    def _():
        for x in range(width):
            part = pl.ds(x * cells, cells)
            c_high[:, part], c_low[:, part] = split(colls[x][...])

    gain = (
        dot(b_high[...], c_high[...]) + dot(b_high[...], c_low[...]) + dot(b_low[...], c_high[...])
    )
    for x in range(width):
        moved = jnp.where(i < blocks, lows[x][...], ups[x][...])
        value = moved + HALF_STEP * fluid[x : x + 1, :] * gain[:, x * cells : (x + 1) * cells]
        out_ref[pl.ds(x, rows, stride=width), :] = value


def finish(lows, ups, colls, turned, fluid):
    half, cells = lows[0].shape
    modes = colls[0].shape[0]
    width = len(lows)
    size = 2 * BLOCK if half % (2 * BLOCK) == 0 else BLOCK
    blocks = half // size
    return pl.pallas_call(
        functools.partial(finish_kernel, blocks, width),
        grid=(2 * blocks,),
        in_specs=[pl.BlockSpec((size, cells), lambda i: (jnp.minimum(i, blocks - 1), 0))] * width
        + [pl.BlockSpec((size, cells), lambda i: (jnp.maximum(i - blocks, 0), 0))] * width
        + [pl.BlockSpec((modes, cells), lambda i: (0, 0))] * width
        + [pl.BlockSpec((size, modes), lambda i: (i, 0))] * 2
        + [pl.BlockSpec((width, cells), lambda i: (0, 0))],
        out_specs=pl.BlockSpec((size * width, cells), lambda i: (i, 0)),
        out_shape=jax.ShapeDtypeStruct((2 * half * width, cells), jnp.float32),
        scratch_shapes=[pltpu.VMEM((modes, width * cells), jnp.bfloat16)] * 2,
        cost_estimate=pl.CostEstimate(
            flops=12 * half * cells * modes * width,
            bytes_accessed=8 * half * (2 * width * cells + modes),
            transcendentals=0,
        ),
        name="finish",
    )(*lows, *ups, *colls, *turned, fluid)


def tables(following, preceding):
    rows = jnp.arange(following.shape[0], dtype=jnp.int32)

    def one_hot(index):
        return (rows[:, None] == index[None, :]).astype(jnp.bfloat16)

    def twice(index):
        table = one_hot(index)
        return jnp.dot(table, table)

    negative = jnp.concatenate([one_hot(following), twice(following), one_hot(preceding)], axis=1)
    positive = jnp.concatenate([one_hot(preceding), twice(preceding), one_hot(following)], axis=1)
    both = jnp.stack([negative, positive])
    return jnp.concatenate([both, both], axis=1)


def matmul(left, right):
    a_high, a_low = split(left)
    b_high, b_low = split(right)
    return dot(a_high, b_high) + dot(a_high, b_low) + dot(a_low, b_high)


def collide_kernel(n, part_ref, left_ref, right_ref, mixing_ref, out_ref, share, moments, landed, send, recv):
    me = lax.axis_index("vel")
    rows = part_ref.shape[0] // n
    own = pl.ds(pl.multiple_of(me * rows, rows), rows)
    peers = [lax.rem(me + k, n) for k in range(1, n)]

    barrier = pltpu.get_barrier_semaphore()
    for peer in peers:
        pl.semaphore_signal(
            barrier, inc=1, device_id={"vel": peer}, device_id_type=pl.DeviceIdType.MESH
        )
    pl.semaphore_wait(barrier, n - 1)

    def total(phase, source, target):
        def copies(step, piece):
            made = []
            for k, peer in enumerate(peers):
                from_ref, to_ref = piece(k, peer)
                made.append(
                    pltpu.make_async_remote_copy(
                        src_ref=from_ref,
                        dst_ref=to_ref,
                        send_sem=send.at[phase + step, k],
                        recv_sem=recv.at[phase + step, k],
                        device_id={"vel": peer},
                        device_id_type=pl.DeviceIdType.MESH,
                    )
                )
            for copy in made:
                copy.start()
            for copy in made:
                copy.wait()

        copies(
            0,
            lambda k, peer: (
                source.at[pl.ds(pl.multiple_of(peer * rows, rows), rows)],
                landed.at[phase // 2, k],
            ),
        )
        added = source[own, :]
        for k in range(n - 1):
            added = added + landed[phase // 2, k]
        target[own, :] = added
        copies(1, lambda k, peer: (target.at[own], target.at[own]))

    total(0, part_ref, moments)
    value = moments[...]
    product = matmul(left_ref[...], value) * matmul(right_ref[...], value)
    share[...] = matmul(mixing_ref[...], product)
    total(2, share, out_ref)


def collide(part, left, right, mixing):
    n = lax.axis_size("vel")
    modes, cells = part.shape
    f32 = jnp.float32
    return pl.pallas_call(
        functools.partial(collide_kernel, n),
        in_specs=[pl.BlockSpec(memory_space=pltpu.VMEM)] * 4,
        out_specs=pl.BlockSpec(memory_space=pltpu.VMEM),
        out_shape=jax.ShapeDtypeStruct((modes, cells), f32),
        scratch_shapes=[
            pltpu.VMEM((modes, cells), f32),
            pltpu.VMEM((modes, cells), f32),
            pltpu.VMEM((2, n - 1, modes // n, cells), f32),
            pltpu.SemaphoreType.DMA((4, n - 1)),
            pltpu.SemaphoreType.DMA((4, n - 1)),
        ],
        compiler_params=pltpu.CompilerParams(
            collective_id=0, has_side_effects=True, vmem_limit_bytes=24 << 20
        ),
        cost_estimate=pl.CostEstimate(
            flops=40 * modes * cells * modes, bytes_accessed=16 * modes * modes, transcendentals=0
        ),
        name="collide",
    )(part, left, right, mixing)


def on_device(dist, basis, left_factor, right_factor, mixing, next_cell, prev_cell, cell_kind):
    per_device, width, extent_y = dist.shape
    half = per_device // 2
    total = per_device * lax.axis_size("vel")
    owner = jnp.reshape(lax.axis_index("vel"), (1,)).astype(jnp.int32)
    fluid = (1 - cell_kind).astype(jnp.float32)
    last = width - 1

    field = dist.reshape(per_device * width, extent_y)
    up = dict(enumerate(columns(field, width, half, True)))
    field, up[0] = lax.optimization_barrier((field, up[0]))
    low = dict(enumerate(columns(field, width, half, False)))
    split_basis = prepare(basis)
    turned = split_basis[2:]
    split_basis = split_basis[:2]
    table = [tables(next_cell[x], prev_cell[x]) for x in range(width)]

    plan = [
        (up, last, -1, 1),
        (low, 0, width, -1),
        (up, last - 1, -2, 1),
        (low, last, -1, 1),
        (low, 1, width + 1, -1),
    ]
    piece = max(half // LAST_PIECES // BLOCK, 1) * BLOCK
    pieces = range(0, half, piece)
    order = list(range(1, last)) + [0, last]
    waiting = [(upper, x) for upper in (False, True) for x in order]
    moved, sums, collision = {}, {}, {}
    token = owner

    def held(value):
        return lax.optimization_barrier((value, token))[0]

    def send(i, after=None):
        if i < len(plan):
            side, x, to, by = plan[i]
            sent = side[x]
        else:
            start = pieces[i - len(plan)]
            sent, by = up[0][start : start + piece], -1
        if after is not None:
            sent = lax.optimization_barrier((sent, after))[0]
        return shifted(sent, by)

    def step(upper, x, *columns, **more):
        return transport(
            upper, held(owner), total, *columns, split_basis, table[x], fluid[x : x + 1], **more
        )

    count = len(plan) + len(pieces)
    flying = [send(0), send(1)]
    for i in range(count + 1):
        if i > 0:
            landed = held(flying[i - 1])
            for _ in range(2 if i == 1 else 1):
                if len(flying) < count:
                    flying.append(send(len(flying), landed))
            if i <= len(plan):
                side, x, to, by = plan[i - 1]
                side[to] = landed
            else:
                start = pieces[i - 1 - len(plan)]
                before = (token, moved[True, last]) if start else ()
                moved[True, last], token = step(
                    True,
                    last,
                    *(up[last - k] for k in (2, 1, 0)),
                    landed,
                    first=start // BLOCK,
                    before=before,
                )
        for upper, x in list(waiting):
            side = up if upper else low
            needs = (x - 2, x - 1, x, x + 1) if upper else (x + 2, x + 1, x, x - 1)
            if any(need not in side for need in needs):
                continue
            waiting.remove((upper, x))
            moved[upper, x], part = step(upper, x, *(side[need] for need in needs))
            token = part
            if x not in sums:
                sums[x] = part
                continue
            collision[x] = collide(held(sums[x] + part), left_factor, right_factor, mixing)
            token = collision[x]
    collision[last] = collide(sums[last] + token, left_factor, right_factor, mixing)

    out = finish(
        [moved[False, x] for x in range(width)],
        [moved[True, x] for x in range(width)],
        [collision[x] for x in range(width)],
        turned,
        fluid,
    )
    return out.reshape(dist.shape)


def solution(mesh):
    in_specs = (
        P("vel", "cells", None),
        P(None, "vel"),
        P("vel", None),
        P("vel", None),
        P(None, "vel"),
        P("cells", None),
        P("cells", None),
        P("cells", None),
    )
    out_specs = P("vel", "cells", None)
    return jax.shard_map(
        on_device, mesh=mesh, in_specs=in_specs, out_specs=out_specs, check_vma=False
    )
```
